32 devices in a mesh: kvh: 4 (over y, x), seq: 8 (over z, core).
Axes of the slice: x: 2, y: 2, z: 4, core: 2. Of those that a mesh axis runs over, the one named last changes fastest.
Arguments:
- queries: bfloat16 [4, 128, 128], P(None, 'kvh'), may hold values from -256 to 256
- keys: bfloat16 [4, 8, 1024, 128], P(None, 'kvh', 'seq'), may hold values from -6 to 6
- values: bfloat16 [4, 8, 1024, 128], P(None, 'kvh', 'seq'), may hold values from -6 to 6
- lengths: int32 [4, 8], P(None, 'seq'), may hold values from 2 to 128
- hidden_in: bfloat16 [4, 16384], P(None, ('kvh', 'seq')), may hold values from -10 to 10
- out_weight: bfloat16 [16384, 16384], P(('kvh', 'seq')), may hold values from -1 to 1
- norm_gain: bfloat16 [16384], replicated, may hold values from 0.3984375 to 1.59375
Outputs:
- attended: bfloat16 [4, 16384], P(None, ('kvh', 'seq'))
- normed: bfloat16 [4, 16384], P(None, ('kvh', 'seq'))
The draws below stay inside these ranges and needn't reach their ends.
All inputs are finite; a program needn't handle non-finite values.
Results may differ from the reference program's by a relative error of at most 0.006.
Values may be sent and summed in bfloat16 or wider, within the bound.
A program may use at most 64 MiB of HBM per device.

```python
import jax
import jax.numpy as jnp
from jax import lax

D = 16384
HEADS = 128
KV = 8
HD = 128
ROWS = 4
TOK_DEV = 128
TOKENS = 1024
N_SEQ = 8


def pair_draw(key):
    base = jax.random.fold_in(key, 23)
    key_query = jax.random.fold_in(base, 0)
    key_cache = jax.random.fold_in(base, 1)
    key_loud = jax.random.fold_in(base, 3)
    group_size = HEADS // KV
    queries = jnp.clip(jax.random.normal(key_query, (ROWS, HEADS, HD), jnp.float32), -6.0, 6.0)
    loud_head = jax.random.randint(key_loud, (ROWS, KV), 1, group_size)
    member = jnp.arange(group_size, dtype=jnp.int32)[None, None, :] == loud_head[:, :, None]
    boost_scale = jnp.where(member, 32.0, 1.0).astype(jnp.float32)
    queries = (queries.reshape(ROWS, KV, group_size, HD) * boost_scale[..., None]).reshape(ROWS, HEADS, HD)
    cached = jnp.clip(jax.random.normal(key_cache, (ROWS, KV, TOKENS, HD), jnp.float32), -6.0, 6.0)
    return (queries, cached)


def draw_queries(key, part):
    return pair_draw(key)[0].astype(jnp.bfloat16)


def draw_keys(key, part):
    return pair_draw(key)[1].astype(jnp.bfloat16)


def draw_hidden_in(key, part):
    base = jax.random.fold_in(key, 41)
    raw = jnp.clip(jax.random.normal(base, (ROWS, D), jnp.float32), -6.0, 6.0)
    ladder = jnp.power(3.0, jnp.arange(D, dtype=jnp.float32) / D)
    ramp = 0.15 * ladder
    return (raw * ramp[None, :]).astype(jnp.bfloat16)


def with_ends(array, key, smallest, high):
    longest = array.shape.index(max(array.shape))
    spots = []
    for shift in (0, 1):
        where = [jax.random.randint(jax.random.fold_in(key, axis), (), 0, length) for axis, length in enumerate(array.shape)]
        where[longest] = (where[longest] + shift) % array.shape[longest]
        spots.append(tuple(where))
    return array.at[spots[0]].set(smallest).at[spots[1]].set(high)


def with_spikes(array, stream_key, source, target, shards_of, factor):
    def block_of(dim):
        return (jnp.arange(array.shape[dim]) // (array.shape[dim] // shards_of)).reshape((-1,) + (1,) * (array.ndim - 1 - dim))

    one_side = jax.random.permutation(stream_key, shards_of)[block_of(target)]
    second = (block_of(target) + shards_of // 2) % shards_of
    return jnp.where((block_of(source) == one_side) | (block_of(source) == second), factor * array, array)


def shard_levels(key, shape, cuts, low, largest):
    def one(dim, shards_of):
        steps = jax.random.uniform(jax.random.fold_in(jax.random.fold_in(key, 6), dim), (shards_of,), jnp.float32, low / len(cuts), largest / len(cuts))
        return jnp.repeat(jnp.exp(steps), shape[dim] // shards_of).reshape((-1,) + (1,) * (len(shape) - dim - 1))

    factor_of = one(*cuts[0])
    for cut in cuts[1:]:
        factor_of = factor_of * one(*cut)
    return factor_of


def normal_values(rng, dims, deviation, reach, shards=(), held_as=jnp.bfloat16):
    factor_of = shard_levels(rng, dims, shards, -0.22, 0.18) if shards else 1.0
    result = jax.random.normal(rng, dims, jnp.float32) * deviation * factor_of
    return jnp.minimum(jnp.maximum(result, -reach), reach).astype(held_as)


def heavy_noise(own_key, shape, spread, bound, cuts, heavy, held_as=jnp.bfloat16):
    drawn = spread * jax.random.normal(own_key, shape, jnp.float32)
    if cuts:
        drawn = drawn * shard_levels(own_key, shape, cuts, -0.22, 0.18)
    return jnp.clip(with_spikes(drawn, jax.random.fold_in(own_key, 3), *heavy), -bound, bound).astype(held_as)


def setup_inputs(seed: int = 0) -> dict:
    arg_keys = jax.random.split(jax.random.key(seed), 8)
    queries = draw_queries(jax.random.fold_in(arg_keys[7], 71), 0)
    keys = draw_keys(jax.random.fold_in(arg_keys[7], 71), 0)
    values = normal_values(arg_keys[2], (ROWS, KV, TOKENS, HD), 1.0, 6.0, ((1, 4), (2, 8)))
    lengths = with_ends(jax.random.randint(arg_keys[3], (ROWS, N_SEQ), 2, TOK_DEV + 1), jax.random.fold_in(arg_keys[3], 1), 2, TOK_DEV).astype(jnp.int32)
    hidden_in = draw_hidden_in(jax.random.fold_in(arg_keys[7], 71), 0)
    out_weight = heavy_noise(arg_keys[5], (HEADS * HD, D), HD ** -0.5, 1.0, ((0, 32),), (0, 1, 32, 2.75))
    norm_gain = jnp.clip(1.0 + 0.12 * jax.random.normal(arg_keys[6], (D,), jnp.float32), 0.3984375, 1.59375).astype(jnp.bfloat16)
    return {"queries": queries, "keys": keys, "values": values, "lengths": lengths, "hidden_in": hidden_in, "out_weight": out_weight, "norm_gain": norm_gain}


def reference(queries, keys, values, lengths, hidden_in, out_weight, norm_gain):
    group_size = HEADS // KV
    shard_count = TOKENS // TOK_DEV
    query_grid = queries.astype(jnp.float32).reshape(ROWS, KV, group_size, HD)

    def one_shard(index):
        offset = (index * TOK_DEV).astype(jnp.int32)
        key_block = lax.dynamic_slice_in_dim(keys, offset, TOK_DEV, 2).astype(jnp.float32)
        value_block = lax.dynamic_slice_in_dim(values, offset, TOK_DEV, 2).astype(jnp.float32)
        scores = jnp.einsum('rkgd,rktd->rkgt', query_grid, key_block) * HD ** (-0.5)
        limit = lengths[:, index]
        valid = (jnp.arange(TOK_DEV, dtype=jnp.int32)[None, :] < limit[:, None])[:, None, None, :]
        peak_here = lax.optimization_barrier(jnp.max(jnp.where(valid, scores, -jnp.inf), axis=-1))
        probs = jnp.exp(jnp.where(valid, scores - peak_here[..., None], -jnp.inf)).astype(jnp.bfloat16)
        probs_wide = probs.astype(jnp.float32)
        weight_here = lax.optimization_barrier(jnp.sum(probs_wide, axis=-1))
        partial_value = jnp.einsum('rkgt,rktd->rkgd', probs_wide, value_block)
        return (peak_here, weight_here, partial_value)
    peaks, weights, partials = lax.map(one_shard, jnp.arange(shard_count, dtype=jnp.int32))
    highest = lax.optimization_barrier(jnp.max(peaks, axis=0))
    factor = jnp.exp(peaks - highest)
    numer = lax.optimization_barrier(jnp.sum(factor[..., None] * partials, axis=0))
    denom = lax.optimization_barrier(jnp.sum(factor * weights, axis=0))
    attention = (numer / denom[..., None]).reshape(ROWS, HEADS * HD).astype(jnp.bfloat16)
    projected = jnp.dot(attention, out_weight, preferred_element_type=jnp.float32)
    attended = (hidden_in.astype(jnp.float32) + projected).astype(jnp.bfloat16)
    stream = attended.astype(jnp.float32)
    mean_sq = lax.optimization_barrier(jnp.mean(stream * stream, axis=1, keepdims=True))
    normed = (stream * lax.rsqrt(mean_sq + 1e-05) * norm_gain.astype(jnp.float32)).astype(jnp.bfloat16)
    return (attended, normed)
```

```python
import functools

import jax
import jax.numpy as jnp
from jax import lax
from jax.experimental import pallas as pl
from jax.experimental.pallas import tpu as pltpu
from jax.sharding import PartitionSpec as P

MESH = pl.DeviceIdType.MESH
LANES = 128


def fused_kernel(dims, q_hbm, k_hbm, v_hbm, len_ref, hid_hbm, w_hbm, gain_ref, att_ref, norm_ref,
                 qv, kv, vv, hv, wv, send_a, recv_a, out_a, send_b, recv_b, send_c, recv_c,
                 in_sem, w_sem, sa_sem, ra_sem, sb_sem, rb_sem, sc_sem, rc_sem):
    n_kvh, n_seq, rows, heads, hd, groups, positions, width = dims
    n = n_kvh * n_seq
    per_group = heads // groups
    own_heads = width // hd
    dests = per_group // own_heads
    m = rows * own_heads
    half = m // 2
    quarter = LANES // 4
    kvh, seq = lax.axis_index("kvh"), lax.axis_index("seq")

    def peer(a, b):
        return lax.rem(kvh + a, n_kvh), lax.rem(seq + b, n_seq)

    seq_order = sorted(range(n_seq), key=lambda b: -min(b, n_seq - b))
    order = [(a, b) for b in seq_order for a in list(range(1, n_kvh)) + [0]]

    barrier = pltpu.get_barrier_semaphore()
    for a, b in order:
        if a or b:
            pl.semaphore_signal(barrier, inc=1, device_id=peer(a, b), device_id_type=MESH)

    loads = [pltpu.make_async_copy(s, d, in_sem.at[i]) for i, (s, d) in enumerate(
        [(q_hbm, qv), (k_hbm, kv), (v_hbm, vv), (hid_hbm, hv)])]
    for load in loads:
        load.start()
    w_loads = []
    for slot, (a, b) in enumerate(order):
        pa, pb = peer(a, b)
        col = pl.multiple_of((pa * n_seq + pb) * width, width)
        load = pltpu.make_async_copy(w_hbm.at[:, pl.ds(col, width)], wv.at[slot], w_sem.at[slot])
        load.start()
        w_loads.append(load)

    loads[0].wait()
    loads[1].wait()
    loads[2].wait()
    lane = lax.broadcasted_iota(jnp.int32, (per_group, LANES), 1)
    position = lax.broadcasted_iota(jnp.int32, (per_group, positions), 1)
    for g in range(groups):
        stats = []
        for r in range(rows):
            scores = lax.dot_general(qv[r, g * per_group:(g + 1) * per_group, :], kv[r, g],
                                     (((1,), (1,)), ((), ())),
                                     preferred_element_type=jnp.float32) * hd ** (-0.5)
            valid = position < len_ref[r, 0]
            peak = jnp.max(jnp.where(valid, scores, -jnp.inf), axis=1, keepdims=True)
            probs = jnp.exp(jnp.where(valid, scores - peak, -jnp.inf)).astype(jnp.bfloat16)
            weight = jnp.sum(probs.astype(jnp.float32), axis=1, keepdims=True)
            part = jnp.dot(probs, vv[r, g], preferred_element_type=jnp.float32)
            stats.append((peak, weight))
            for j in range(dests):
                send_a[g * dests + j, r * own_heads:(r + 1) * own_heads, :] = (
                    part[j * own_heads:(j + 1) * own_heads, :])
        for rr in range(rows // 2):
            low, high = stats[rr], stats[rr + rows // 2]
            tile = jnp.where(lane < 2 * quarter,
                             jnp.where(lane < quarter, low[0], low[1]),
                             jnp.where(lane < 3 * quarter, high[0], high[1]))
            for j in range(dests):
                send_a[g * dests + j, m + rr * own_heads:m + (rr + 1) * own_heads, :] = (
                    tile[j * own_heads:(j + 1) * own_heads, :])

    pl.semaphore_wait(barrier, n - 1)
    copies = []
    for b in seq_order:
        if b:
            pa, pb = peer(0, b)
            copy = pltpu.make_async_remote_copy(
                src_ref=send_a.at[pb], dst_ref=recv_a.at[b], send_sem=sa_sem.at[b],
                recv_sem=ra_sem.at[b], device_id=(pa, pb), device_id_type=MESH)
            copy.start()
            copies.append(copy)
    recv_a[0] = send_a[seq]
    for copy in copies:
        copy.wait_recv()

    tiles = [recv_a[b, m:m + half, :] for b in range(n_seq)]
    top = functools.reduce(jnp.maximum, tiles)
    scales = [jnp.exp(tile - top) for tile in tiles]
    denom = functools.reduce(jnp.add, [
        scale * pltpu.roll(tile, LANES - quarter, 1) for scale, tile in zip(scales, tiles)])
    for h in range(2):
        at = h * 2 * quarter
        numer = functools.reduce(jnp.add, [
            scales[b][:, at:at + 1] * recv_a[b, h * half:(h + 1) * half, :] for b in range(n_seq)])
        out_a[h * half:(h + 1) * half, :] = numer / denom[:, at:at + 1]
    attention = jnp.concatenate(
        [out_a[pl.ds(i, rows, stride=own_heads), :] for i in range(own_heads)], axis=1
    ).astype(jnp.bfloat16)

    own = None
    for slot, (a, b) in enumerate(order):
        w_loads[slot].wait()
        product = jnp.dot(attention, wv[slot], preferred_element_type=jnp.float32)
        if a == 0 and b == 0:
            own = product
            continue
        send_b[slot] = product.astype(send_b.dtype)
        copy = pltpu.make_async_remote_copy(
            src_ref=send_b.at[slot], dst_ref=recv_b.at[slot], send_sem=sb_sem.at[slot],
            recv_sem=rb_sem.at[slot], device_id=peer(a, b), device_id_type=MESH)
        copy.start()
        copies.append(copy)
    loads[3].wait()
    total = own + hv[...].astype(jnp.float32)
    for copy in copies[n_seq - 1:]:
        copy.wait_recv()
    for slot in range(n - 1):
        total = total + recv_b[slot].astype(jnp.float32)
    attended = total.astype(jnp.bfloat16)
    att_ref[...] = attended
    stream = attended.astype(jnp.float32)
    squares = jnp.sum(stream * stream, axis=1, keepdims=True)
    lane_one = lax.broadcasted_iota(jnp.int32, (1, LANES), 1)
    packed = jnp.zeros((1, LANES), jnp.float32)
    share = LANES // rows
    for r in range(rows):
        packed = jnp.where(lane_one // share == r, squares[r:r + 1, :], packed)
    send_c[...] = packed
    last = []
    for slot, (a, b) in enumerate(order):
        if a or b:
            copy = pltpu.make_async_remote_copy(
                src_ref=send_c, dst_ref=recv_c.at[slot], send_sem=sc_sem.at[slot],
                recv_sem=rc_sem.at[slot], device_id=peer(a, b), device_id_type=MESH)
            copy.start()
            last.append(copy)
    gain_wide = gain_ref[...].astype(jnp.float32)
    for copy in last:
        copy.wait_recv()
    for slot in range(n - 1):
        packed = packed + recv_c[slot]
    scale = lax.rsqrt(packed / (n * width) + 1e-05)
    for r in range(rows):
        norm_ref[r:r + 1, :] = (
            stream[r:r + 1, :] * scale[:, r * share:r * share + 1] * gain_wide
        ).astype(jnp.bfloat16)
    for copy in copies + last:
        copy.wait_send()


def fused_body(queries, keys, values, lengths, hidden_in, out_weight, norm_gain):
    rows, heads, hd = queries.shape
    groups, positions = keys.shape[1], keys.shape[2]
    n_kvh, n_seq = lax.axis_size("kvh"), lax.axis_size("seq")
    n = n_kvh * n_seq
    width = hidden_in.shape[1]
    own_heads = width // hd
    m = rows * own_heads
    message = m + m // 2
    start = lax.axis_index(("kvh", "seq")) * width
    gain = lax.dynamic_slice_in_dim(norm_gain, start, width, 0).reshape(1, width)
    dims = (n_kvh, n_seq, rows, heads, hd, groups, positions, width)
    anywhere = pl.BlockSpec(memory_space=pl.ANY)
    vmem = pl.BlockSpec(memory_space=pltpu.VMEM)
    out = jax.ShapeDtypeStruct((rows, width), jnp.bfloat16)
    return pl.pallas_call(
        functools.partial(fused_kernel, dims),
        out_shape=(out, out),
        in_specs=[anywhere, anywhere, anywhere, pl.BlockSpec(memory_space=pltpu.SMEM), anywhere,
                  anywhere, vmem],
        out_specs=(vmem, vmem),
        scratch_shapes=[
            pltpu.VMEM(queries.shape, queries.dtype),
            pltpu.VMEM(keys.shape, keys.dtype),
            pltpu.VMEM(values.shape, values.dtype),
            pltpu.VMEM(hidden_in.shape, hidden_in.dtype),
            pltpu.VMEM((n, out_weight.shape[0], width), out_weight.dtype),
            pltpu.VMEM((n_seq, message, hd), jnp.float32),
            pltpu.VMEM((n_seq, message, hd), jnp.float32),
            pltpu.VMEM((m, hd), jnp.float32),
            pltpu.VMEM((n, rows, width), jnp.bfloat16),
            pltpu.VMEM((n, rows, width), jnp.bfloat16),
            pltpu.VMEM((1, LANES), jnp.float32),
            pltpu.VMEM((n, 1, LANES), jnp.float32),
            pltpu.SemaphoreType.DMA((4,)),
            pltpu.SemaphoreType.DMA((n,)),
            pltpu.SemaphoreType.DMA((n_seq,)),
            pltpu.SemaphoreType.DMA((n_seq,)),
            pltpu.SemaphoreType.DMA((n,)),
            pltpu.SemaphoreType.DMA((n,)),
            pltpu.SemaphoreType.DMA((n,)),
            pltpu.SemaphoreType.DMA((n,)),
        ],
        compiler_params=pltpu.CompilerParams(
            collective_id=0, has_side_effects=True, vmem_limit_bytes=48 * 1024 * 1024),
    )(queries, keys, values, lengths, hidden_in, out_weight, gain)


def fits(queries, keys, hidden_in, out_weight):
    rows, heads, hd = queries.shape
    groups, width = keys.shape[1], hidden_in.shape[1]
    return (hd == LANES and width % hd == 0 and (heads // groups) % max(width // hd, 1) == 0
            and rows % 2 == 0 and (rows * (width // hd)) % 16 == 0 and LANES % rows == 0
            and out_weight.shape[0] == width and out_weight.size * 2 <= 32 * 1024 * 1024)


def merged(shard, axis, combine):
    everything = jax.tree.map(lambda part: lax.all_gather(part, axis), shard)
    leading = jax.tree.map(lambda part: part[0], everything)

    def lap(k, so_far):
        return combine(so_far, jax.tree.map(lambda part: part[k], everything))

    return lax.fori_loop(1, lax.axis_size(axis), lap, leading)


def softmax_pair(first, second):
    highest = jnp.maximum(first[0], second[0])
    first_scale = jnp.exp(first[0] - highest)
    second_scale = jnp.exp(second[0] - highest)
    weight_total = first[1] * first_scale + second[1] * second_scale
    output_total = first[2] * first_scale[..., None] + second[2] * second_scale[..., None]
    return (highest, weight_total, output_total)


def body(queries, keys, values, lengths, hidden_in, out_weight, norm_gain):
    rows, heads_here, head_dim = queries.shape
    groups = keys.shape[1]
    positions = keys.shape[2]
    per_group = heads_here // groups
    query_grid = queries.reshape(rows, groups, per_group, head_dim)
    scores = jnp.einsum(
        "rkgd,rktd->rkgt", query_grid, keys, preferred_element_type=jnp.float32
    ) * head_dim ** (-0.5)
    valid = (jnp.arange(positions, dtype=jnp.int32)[None, :] < lengths)[:, None, None, :]
    peak_here = jnp.max(jnp.where(valid, scores, -jnp.inf), axis=-1)
    probs = jnp.exp(jnp.where(valid, scores - peak_here[..., None], -jnp.inf)).astype(jnp.bfloat16)
    weight_here = jnp.sum(probs, axis=-1, dtype=jnp.float32)
    partial_value = jnp.einsum("rkgt,rktd->rkgd", probs, values, preferred_element_type=jnp.float32)
    feature_width = heads_here * head_dim // lax.axis_size("seq")
    feature_start = lax.axis_index("seq") * feature_width
    highest, weight_total, output_total = merged(
        (peak_here, weight_here, partial_value), "seq", softmax_pair
    )
    whole_out = (output_total / weight_total[..., None]).reshape(rows, heads_here * head_dim)
    attention = lax.dynamic_slice_in_dim(whole_out, feature_start, feature_width, 1)
    attention = attention.astype(jnp.bfloat16)
    projected = jnp.dot(attention, out_weight, preferred_element_type=jnp.float32)
    slice_width = hidden_in.shape[1]
    slice_start = lax.axis_index(("kvh", "seq")) * slice_width
    gain_wide = norm_gain.astype(jnp.float32)
    projected_all = lax.psum(projected, ("kvh", "seq"))
    residual = lax.all_gather(hidden_in, ("kvh", "seq"), axis=1, tiled=True)
    stream_all = (residual.astype(jnp.float32) + projected_all).astype(jnp.bfloat16)
    stream_wide = stream_all.astype(jnp.float32)
    mean_square = jnp.mean(stream_wide * stream_wide, axis=1, keepdims=True)
    normed_all = (stream_wide * lax.rsqrt(mean_square + 1e-05) * gain_wide[None, :]).astype(
        jnp.bfloat16
    )
    attended = lax.dynamic_slice_in_dim(stream_all, slice_start, slice_width, 1)
    normed = lax.dynamic_slice_in_dim(normed_all, slice_start, slice_width, 1)
    return (attended, normed)


def either_body(queries, keys, values, lengths, hidden_in, out_weight, norm_gain):
    chosen = fused_body if fits(queries, keys, hidden_in, out_weight) else body
    return chosen(queries, keys, values, lengths, hidden_in, out_weight, norm_gain)


def solution(mesh):
    placed = (
        P(None, "kvh", None),
        P(None, "kvh", "seq", None),
        P(None, "kvh", "seq", None),
        P(None, "seq"),
        P(None, ("kvh", "seq")),
        P(("kvh", "seq"), None),
        P(),
    )
    return jax.shard_map(
        either_body,
        mesh=mesh,
        in_specs=placed,
        out_specs=(P(None, ("kvh", "seq")), P(None, ("kvh", "seq"))),
        check_vma=False,
    )
```

```python
import functools

import jax
import jax.numpy as jnp
from jax import lax
from jax.experimental import pallas as pl
from jax.experimental.pallas import tpu as pltpu
from jax.sharding import PartitionSpec as P

MESH = pl.DeviceIdType.MESH
LANES = 128


def fused_kernel(dims, q_hbm, k_hbm, v_hbm, len_ref, hid_hbm, w_hbm, gain_hbm, out_ref,
                 qv, kv, vv, hv, gv, wv, send_a, recv_a, out_a, send_b, recv_b, send_c, recv_c,
                 in_sem, w_sem, sa_sem, ra_sem, sb_sem, rb_sem, sc_sem, rc_sem):
    n_kvh, n_seq, rows, heads, hd, groups, positions, width = dims
    n = n_kvh * n_seq
    per_group = heads // groups
    own_heads = width // hd
    dests = per_group // own_heads
    m = rows * own_heads
    half = m // 2
    quarter = LANES // 4
    kvh, seq = lax.axis_index("kvh"), lax.axis_index("seq")

    def flip(index, mask):
        bits = mask.bit_length()
        low = sum(lax.rem(index // (1 << i) + (mask >> i & 1), 2) * (1 << i) for i in range(bits))
        return (index // (1 << bits)) * (1 << bits) + low

    def peer(a, b):
        return flip(kvh, a), flip(seq, b)

    def hops(pair):
        return (pair[0].bit_count() + (pair[1] >> 1)), pair[0], pair[1]

    order = sorted(((a, b) for a in range(n_kvh) for b in range(n_seq)), key=hops, reverse=True)
    seq_order = sorted(range(n_seq), reverse=True)

    barrier = pltpu.get_barrier_semaphore()
    for a, b in order:
        if a or b:
            pl.semaphore_signal(barrier, inc=1, device_id=peer(a, b), device_id_type=MESH)

    loads = [pltpu.make_async_copy(s, d, in_sem.at[i]) for i, (s, d) in enumerate(
        [(q_hbm, qv), (k_hbm, kv), (v_hbm, vv), (hid_hbm, hv),
         (gain_hbm.at[pl.ds(pl.multiple_of((kvh * n_seq + seq) * width, width), width)], gv)])]
    for load in loads:
        load.start()
    w_loads = []
    for slot, (a, b) in enumerate(order):
        pa, pb = peer(a, b)
        col = pl.multiple_of((pa * n_seq + pb) * width, width)
        load = pltpu.make_async_copy(w_hbm.at[:, pl.ds(col, width)], wv.at[slot], w_sem.at[slot])
        load.start()
        w_loads.append(load)

    loads[0].wait()
    loads[1].wait()
    loads[2].wait()
    lane = lax.broadcasted_iota(jnp.int32, (per_group, LANES), 1)
    position = lax.broadcasted_iota(jnp.int32, (per_group, positions), 1)
    for g in range(groups):
        stats = []
        for r in range(rows):
            scores = lax.dot_general(qv[r, g * per_group:(g + 1) * per_group, :], kv[r, g],
                                     (((1,), (1,)), ((), ())),
                                     preferred_element_type=jnp.float32) * hd ** (-0.5)
            valid = position < len_ref[0, r]
            peak = jnp.max(jnp.where(valid, scores, -jnp.inf), axis=1, keepdims=True)
            probs = jnp.exp(jnp.where(valid, scores - peak, -jnp.inf)).astype(jnp.bfloat16)
            weight = jnp.sum(probs.astype(jnp.float32), axis=1, keepdims=True)
            part = jnp.dot(probs, vv[r, g], preferred_element_type=jnp.float32)
            stats.append((peak, weight))
            for j in range(dests):
                send_a[g * dests + j, r * own_heads:(r + 1) * own_heads, :] = (
                    part[j * own_heads:(j + 1) * own_heads, :])
        for rr in range(rows // 2):
            low, high = stats[rr], stats[rr + rows // 2]
            tile = jnp.where(lane < 2 * quarter,
                             jnp.where(lane < quarter, low[0], low[1]),
                             jnp.where(lane < 3 * quarter, high[0], high[1]))
            for j in range(dests):
                send_a[g * dests + j, m + rr * own_heads:m + (rr + 1) * own_heads, :] = (
                    tile[j * own_heads:(j + 1) * own_heads, :])

    pl.semaphore_wait(barrier, n - 1)
    copies = []
    for b in seq_order:
        if b:
            pa, pb = peer(0, b)
            copy = pltpu.make_async_remote_copy(
                src_ref=send_a.at[pb], dst_ref=recv_a.at[b], send_sem=sa_sem.at[b],
                recv_sem=ra_sem.at[b], device_id=(pa, pb), device_id_type=MESH)
            copy.start()
            copies.append(copy)
    recv_a[0] = send_a[seq]
    for copy in copies:
        copy.wait_recv()

    tiles = [recv_a[b, m:m + half, :] for b in range(n_seq)]
    top = functools.reduce(jnp.maximum, tiles)
    scales = [jnp.exp(tile - top) for tile in tiles]
    denom = functools.reduce(jnp.add, [
        scale * pltpu.roll(tile, LANES - quarter, 1) for scale, tile in zip(scales, tiles)])
    for h in range(2):
        at = h * 2 * quarter
        numer = functools.reduce(jnp.add, [
            scales[b][:, at:at + 1] * recv_a[b, h * half:(h + 1) * half, :] for b in range(n_seq)])
        out_a[h * half:(h + 1) * half, :] = numer / denom[:, at:at + 1]
    attention = jnp.concatenate(
        [out_a[pl.ds(i, rows, stride=own_heads), :] for i in range(own_heads)], axis=1
    ).astype(jnp.bfloat16)

    own = None
    for slot, (a, b) in enumerate(order):
        w_loads[slot].wait()
        product = jnp.dot(attention, wv[slot], preferred_element_type=jnp.float32)
        if a == 0 and b == 0:
            own = product
            continue
        send_b[slot] = product.astype(send_b.dtype)
        copy = pltpu.make_async_remote_copy(
            src_ref=send_b.at[slot], dst_ref=recv_b.at[slot], send_sem=sb_sem.at[slot],
            recv_sem=rb_sem.at[slot], device_id=peer(a, b), device_id_type=MESH)
        copy.start()
        copies.append(copy)
    loads[3].wait()
    total = own + hv[...].astype(jnp.float32)
    for first in range(0, n - 1, 8):
        group = range(first, min(first + 8, n - 1))
        for slot in group:
            copies[n_seq - 1 + slot].wait_recv()
        for slot in group:
            total = total + recv_b[slot].astype(jnp.float32)
    attended = total.astype(jnp.bfloat16)
    out_ref[0] = attended
    stream = attended.astype(jnp.float32)
    squares = jnp.sum(stream * stream, axis=1, keepdims=True)
    lane_one = lax.broadcasted_iota(jnp.int32, (1, LANES), 1)
    packed = jnp.zeros((1, LANES), jnp.float32)
    share = LANES // rows
    for r in range(rows):
        packed = jnp.where(lane_one // share == r, squares[r:r + 1, :], packed)
    send_c[...] = packed
    last = []
    for slot, (a, b) in enumerate(order):
        if a or b:
            copy = pltpu.make_async_remote_copy(
                src_ref=send_c, dst_ref=recv_c.at[slot], send_sem=sc_sem.at[slot],
                recv_sem=rc_sem.at[slot], device_id=peer(a, b), device_id_type=MESH)
            copy.start()
            last.append(copy)
    loads[4].wait()
    gain_wide = gv[...].astype(jnp.float32).reshape(1, width)
    for copy in last:
        copy.wait_recv()
    for slot in range(n - 1):
        packed = packed + recv_c[slot]
    scale = lax.rsqrt(packed / (n * width) + 1e-05)
    for r in range(rows):
        out_ref[1, r:r + 1, :] = (
            stream[r:r + 1, :] * scale[:, r * share:r * share + 1] * gain_wide
        ).astype(jnp.bfloat16)
    for copy in copies + last:
        copy.wait_send()


def fused_body(queries, keys, values, lengths, hidden_in, out_weight, norm_gain):
    rows, heads, hd = queries.shape
    groups, positions = keys.shape[1], keys.shape[2]
    n_kvh, n_seq = lax.axis_size("kvh"), lax.axis_size("seq")
    n = n_kvh * n_seq
    width = hidden_in.shape[1]
    own_heads = width // hd
    m = rows * own_heads
    message = m + m // 2
    dims = (n_kvh, n_seq, rows, heads, hd, groups, positions, width)
    hbm = pl.BlockSpec(memory_space=pltpu.HBM)
    vmem = pl.BlockSpec(memory_space=pltpu.VMEM)
    both = pl.pallas_call(
        functools.partial(fused_kernel, dims),
        out_shape=jax.ShapeDtypeStruct((2, rows, width), jnp.bfloat16),
        in_specs=[hbm, hbm, hbm, pl.BlockSpec(memory_space=pltpu.SMEM), hbm, hbm, hbm],
        out_specs=vmem,
        scratch_shapes=[
            pltpu.VMEM(queries.shape, queries.dtype),
            pltpu.VMEM(keys.shape, keys.dtype),
            pltpu.VMEM(values.shape, values.dtype),
            pltpu.VMEM(hidden_in.shape, hidden_in.dtype),
            pltpu.VMEM((width,), norm_gain.dtype),
            pltpu.VMEM((n, out_weight.shape[0], width), out_weight.dtype),
            pltpu.VMEM((n_seq, message, hd), jnp.float32),
            pltpu.VMEM((n_seq, message, hd), jnp.float32),
            pltpu.VMEM((m, hd), jnp.float32),
            pltpu.VMEM((n, rows, width), jnp.bfloat16),
            pltpu.VMEM((n, rows, width), jnp.bfloat16),
            pltpu.VMEM((1, LANES), jnp.float32),
            pltpu.VMEM((n, 1, LANES), jnp.float32),
            pltpu.SemaphoreType.DMA((5,)),
            pltpu.SemaphoreType.DMA((n,)),
            pltpu.SemaphoreType.DMA((n_seq,)),
            pltpu.SemaphoreType.DMA((n_seq,)),
            pltpu.SemaphoreType.DMA((n,)),
            pltpu.SemaphoreType.DMA((n,)),
            pltpu.SemaphoreType.DMA((n,)),
            pltpu.SemaphoreType.DMA((n,)),
        ],
        compiler_params=pltpu.CompilerParams(
            collective_id=0, has_side_effects=True, vmem_limit_bytes=67043328),
    )(queries, keys, values, lengths.T, hidden_in, out_weight, norm_gain)
    return both[0], both[1]


def fits(queries, keys, hidden_in, out_weight):
    rows, heads, hd = queries.shape
    groups, width = keys.shape[1], hidden_in.shape[1]
    n_kvh, n_seq = lax.axis_size("kvh"), lax.axis_size("seq")
    return (hd == LANES and n_kvh & (n_kvh - 1) == 0 and n_seq & (n_seq - 1) == 0 and width % hd == 0 and (heads // groups) % max(width // hd, 1) == 0
            and rows % 2 == 0 and (rows * (width // hd)) % 16 == 0 and LANES % rows == 0
            and out_weight.shape[0] == width and out_weight.size * 2 <= 32 * 1024 * 1024)


def merged(shard, axis, combine):
    everything = jax.tree.map(lambda part: lax.all_gather(part, axis), shard)
    leading = jax.tree.map(lambda part: part[0], everything)

    def lap(k, so_far):
        return combine(so_far, jax.tree.map(lambda part: part[k], everything))

    return lax.fori_loop(1, lax.axis_size(axis), lap, leading)


def softmax_pair(first, second):
    highest = jnp.maximum(first[0], second[0])
    first_scale = jnp.exp(first[0] - highest)
    second_scale = jnp.exp(second[0] - highest)
    weight_total = first[1] * first_scale + second[1] * second_scale
    output_total = first[2] * first_scale[..., None] + second[2] * second_scale[..., None]
    return (highest, weight_total, output_total)


def body(queries, keys, values, lengths, hidden_in, out_weight, norm_gain):
    rows, heads_here, head_dim = queries.shape
    groups = keys.shape[1]
    positions = keys.shape[2]
    per_group = heads_here // groups
    query_grid = queries.reshape(rows, groups, per_group, head_dim)
    scores = jnp.einsum(
        "rkgd,rktd->rkgt", query_grid, keys, preferred_element_type=jnp.float32
    ) * head_dim ** (-0.5)
    valid = (jnp.arange(positions, dtype=jnp.int32)[None, :] < lengths)[:, None, None, :]
    peak_here = jnp.max(jnp.where(valid, scores, -jnp.inf), axis=-1)
    probs = jnp.exp(jnp.where(valid, scores - peak_here[..., None], -jnp.inf)).astype(jnp.bfloat16)
    weight_here = jnp.sum(probs, axis=-1, dtype=jnp.float32)
    partial_value = jnp.einsum("rkgt,rktd->rkgd", probs, values, preferred_element_type=jnp.float32)
    feature_width = heads_here * head_dim // lax.axis_size("seq")
    feature_start = lax.axis_index("seq") * feature_width
    highest, weight_total, output_total = merged(
        (peak_here, weight_here, partial_value), "seq", softmax_pair
    )
    whole_out = (output_total / weight_total[..., None]).reshape(rows, heads_here * head_dim)
    attention = lax.dynamic_slice_in_dim(whole_out, feature_start, feature_width, 1)
    attention = attention.astype(jnp.bfloat16)
    projected = jnp.dot(attention, out_weight, preferred_element_type=jnp.float32)
    slice_width = hidden_in.shape[1]
    slice_start = lax.axis_index(("kvh", "seq")) * slice_width
    gain_wide = norm_gain.astype(jnp.float32)
    projected_all = lax.psum(projected, ("kvh", "seq"))
    residual = lax.all_gather(hidden_in, ("kvh", "seq"), axis=1, tiled=True)
    stream_all = (residual.astype(jnp.float32) + projected_all).astype(jnp.bfloat16)
    stream_wide = stream_all.astype(jnp.float32)
    mean_square = jnp.mean(stream_wide * stream_wide, axis=1, keepdims=True)
    normed_all = (stream_wide * lax.rsqrt(mean_square + 1e-05) * gain_wide[None, :]).astype(
        jnp.bfloat16
    )
    attended = lax.dynamic_slice_in_dim(stream_all, slice_start, slice_width, 1)
    normed = lax.dynamic_slice_in_dim(normed_all, slice_start, slice_width, 1)
    return (attended, normed)


def either_body(queries, keys, values, lengths, hidden_in, out_weight, norm_gain):
    chosen = fused_body if fits(queries, keys, hidden_in, out_weight) else body
    return chosen(queries, keys, values, lengths, hidden_in, out_weight, norm_gain)


def solution(mesh):
    placed = (
        P(None, "kvh", None),
        P(None, "kvh", "seq", None),
        P(None, "kvh", "seq", None),
        P(None, "seq"),
        P(None, ("kvh", "seq")),
        P(("kvh", "seq"), None),
        P(),
    )
    return jax.shard_map(
        either_body,
        mesh=mesh,
        in_specs=placed,
        out_specs=(P(None, ("kvh", "seq")), P(None, ("kvh", "seq"))),
        check_vma=False,
    )
```

```python
import functools

import jax
import jax.numpy as jnp
from jax import lax
from jax.experimental import pallas as pl
from jax.experimental.pallas import tpu as pltpu
from jax.sharding import PartitionSpec as P

MESH = pl.DeviceIdType.MESH
LANES = 128
CHUNK = 4


def fused_kernel(dims, q_hbm, k_hbm, v_hbm, len_hbm, hid_hbm, w_hbm, gain_hbm, out_ref,
                 qv, kv, vv, lv, hv, gv, wv, send_a, recv_a, out_a, send_b, recv_b, send_c, recv_c,
                 in_sem, w_sem, sa_sem, ra_sem, sb_sem, rb_sem, sc_sem, rc_sem):
    n_kvh, n_seq, rows, heads, hd, groups, positions, width = dims
    n = n_kvh * n_seq
    per_group = heads // groups
    own_heads = width // hd
    dests = per_group // own_heads
    m = rows * own_heads
    half = m // 2
    quarter = LANES // 4
    kvh, seq = lax.axis_index("kvh"), lax.axis_index("seq")

    def flip(index, mask):
        bits = mask.bit_length()
        low = sum(lax.rem(index // (1 << i) + (mask >> i & 1), 2) * (1 << i) for i in range(bits))
        return (index // (1 << bits)) * (1 << bits) + low

    def peer(a, b):
        return flip(kvh, a), flip(seq, b)

    def hops(pair):
        return (pair[0].bit_count() + (pair[1] >> 1)), pair[0], pair[1]

    order = sorted(((a, b) for a in range(n_kvh) for b in range(n_seq)), key=hops, reverse=True)
    seq_order = sorted(range(n_seq), reverse=True)

    loads = [pltpu.make_async_copy(s, d, in_sem.at[i]) for i, (s, d) in enumerate(
        [(q_hbm, qv), (k_hbm, kv), (v_hbm, vv), (len_hbm, lv), (hid_hbm, hv),
         (gain_hbm.at[pl.ds(pl.multiple_of((kvh * n_seq + seq) * width, width), width)], gv)])]
    for load in loads[:4]:
        load.start()
    barrier = pltpu.get_barrier_semaphore()
    for a, b in order:
        if a or b:
            pl.semaphore_signal(barrier, inc=1, device_id=peer(a, b), device_id_type=MESH)

    for load in loads[4:]:
        load.start()
    w_loads = []
    for slot, (a, b) in enumerate(order):
        pa, pb = peer(a, b)
        col = pl.multiple_of((pa * n_seq + pb) * width, width)
        load = pltpu.make_async_copy(w_hbm.at[:, pl.ds(col, width)], wv.at[slot], w_sem.at[slot])
        load.start()
        w_loads.append(load)

    for load in loads[:4]:
        load.wait()
    lane = lax.broadcasted_iota(jnp.int32, (per_group, LANES), 1)
    position = lax.broadcasted_iota(jnp.int32, (per_group, positions), 1)
    for g in range(groups):
        stats = []
        for r in range(rows):
            scores = lax.dot_general(qv[r, g * per_group:(g + 1) * per_group, :], kv[r, g],
                                     (((1,), (1,)), ((), ())),
                                     preferred_element_type=jnp.float32) * hd ** (-0.5)
            valid = position < lv[0:1, r:r + 1]
            peak = jnp.max(jnp.where(valid, scores, -jnp.inf), axis=1, keepdims=True)
            probs = jnp.exp(jnp.where(valid, scores - peak, -jnp.inf)).astype(jnp.bfloat16)
            weight = jnp.sum(probs.astype(jnp.float32), axis=1, keepdims=True)
            part = jnp.dot(probs, vv[r, g], preferred_element_type=jnp.float32)
            stats.append((peak, weight))
            for j in range(dests):
                send_a[g * dests + j, r * own_heads:(r + 1) * own_heads, :] = (
                    part[j * own_heads:(j + 1) * own_heads, :])
        for rr in range(rows // 2):
            low, high = stats[rr], stats[rr + rows // 2]
            tile = jnp.where(lane < 2 * quarter,
                             jnp.where(lane < quarter, low[0], low[1]),
                             jnp.where(lane < 3 * quarter, high[0], high[1]))
            for j in range(dests):
                send_a[g * dests + j, m + rr * own_heads:m + (rr + 1) * own_heads, :] = (
                    tile[j * own_heads:(j + 1) * own_heads, :])

    pl.semaphore_wait(barrier, n - 1)
    copies = []
    for b in seq_order:
        if b:
            pa, pb = peer(0, b)
            copy = pltpu.make_async_remote_copy(
                src_ref=send_a.at[pb], dst_ref=recv_a.at[b], send_sem=sa_sem.at[b],
                recv_sem=ra_sem.at[b], device_id=(pa, pb), device_id_type=MESH)
            copy.start()
            copies.append(copy)
    recv_a[0] = send_a[seq]
    for copy in copies:
        copy.wait_recv()

    tiles = [recv_a[b, m:m + half, :] for b in range(n_seq)]
    top = functools.reduce(jnp.maximum, tiles)
    scales = [jnp.exp(tile - top) for tile in tiles]
    denom = functools.reduce(jnp.add, [
        scale * pltpu.roll(tile, LANES - quarter, 1) for scale, tile in zip(scales, tiles)])
    for h in range(2):
        at = h * 2 * quarter
        numer = functools.reduce(jnp.add, [
            scales[b][:, at:at + 1] * recv_a[b, h * half:(h + 1) * half, :] for b in range(n_seq)])
        out_a[h * half:(h + 1) * half, :] = numer / denom[:, at:at + 1]
    attention = jnp.concatenate(
        [out_a[pl.ds(i, rows, stride=own_heads), :] for i in range(own_heads)], axis=1
    ).astype(jnp.bfloat16)

    for first in range(0, n, CHUNK):
        slots = range(first, first + CHUNK)
        for slot in slots:
            w_loads[slot].wait()
        products = [jnp.dot(attention, wv[slot], preferred_element_type=jnp.float32)
                    for slot in slots]
        for slot, product in zip(slots, products):
            if slot < n - 1:
                send_b[slot] = product.astype(send_b.dtype)
        for slot in slots:
            if slot < n - 1:
                copy = pltpu.make_async_remote_copy(
                    src_ref=send_b.at[slot], dst_ref=recv_b.at[slot], send_sem=sb_sem.at[slot],
                    recv_sem=rb_sem.at[slot], device_id=peer(*order[slot]), device_id_type=MESH)
                copy.start()
                copies.append(copy)
    own = products[-1]
    loads[4].wait()
    total = own + hv[...].astype(jnp.float32)
    for first in range(0, n - 1, 8):
        group = range(first, min(first + 8, n - 1))
        for slot in group:
            copies[n_seq - 1 + slot].wait_recv()
        for slot in group:
            total = total + recv_b[slot].astype(jnp.float32)
    attended = total.astype(jnp.bfloat16)
    out_ref[0] = attended
    stream = attended.astype(jnp.float32)
    squares = jnp.sum(stream * stream, axis=1, keepdims=True)
    lane_one = lax.broadcasted_iota(jnp.int32, (1, LANES), 1)
    packed = jnp.zeros((1, LANES), jnp.float32)
    share = LANES // rows
    for r in range(rows):
        packed = jnp.where(lane_one // share == r, squares[r:r + 1, :], packed)
    send_c[...] = packed
    last = []
    for slot, (a, b) in enumerate(order):
        if a or b:
            copy = pltpu.make_async_remote_copy(
                src_ref=send_c, dst_ref=recv_c.at[slot], send_sem=sc_sem.at[slot],
                recv_sem=rc_sem.at[slot], device_id=peer(a, b), device_id_type=MESH)
            copy.start()
            last.append(copy)
    loads[5].wait()
    gain_wide = gv[...].astype(jnp.float32).reshape(1, width)
    for copy in last:
        copy.wait_recv()
    for slot in range(n - 1):
        packed = packed + recv_c[slot]
    scale = lax.rsqrt(packed / (n * width) + 1e-05)
    for r in range(rows):
        out_ref[1, r:r + 1, :] = (
            stream[r:r + 1, :] * scale[:, r * share:r * share + 1] * gain_wide
        ).astype(jnp.bfloat16)
    for copy in copies + last:
        copy.wait_send()


def fused_body(queries, keys, values, lengths, hidden_in, out_weight, norm_gain):
    rows, heads, hd = queries.shape
    groups, positions = keys.shape[1], keys.shape[2]
    n_kvh, n_seq = lax.axis_size("kvh"), lax.axis_size("seq")
    n = n_kvh * n_seq
    width = hidden_in.shape[1]
    own_heads = width // hd
    m = rows * own_heads
    message = m + m // 2
    dims = (n_kvh, n_seq, rows, heads, hd, groups, positions, width)
    hbm = pl.BlockSpec(memory_space=pltpu.HBM)
    vmem = pl.BlockSpec(memory_space=pltpu.VMEM)
    both = pl.pallas_call(
        functools.partial(fused_kernel, dims),
        out_shape=jax.ShapeDtypeStruct((2, rows, width), jnp.bfloat16),
        in_specs=[hbm] * 7,
        out_specs=vmem,
        scratch_shapes=[
            pltpu.VMEM(queries.shape, queries.dtype),
            pltpu.VMEM(keys.shape, keys.dtype),
            pltpu.VMEM(values.shape, values.dtype),
            pltpu.VMEM(lengths.T.shape, lengths.dtype),
            pltpu.VMEM(hidden_in.shape, hidden_in.dtype),
            pltpu.VMEM((width,), norm_gain.dtype),
            pltpu.VMEM((n, out_weight.shape[0], width), out_weight.dtype),
            pltpu.VMEM((n_seq, message, hd), jnp.float32),
            pltpu.VMEM((n_seq, message, hd), jnp.float32),
            pltpu.VMEM((m, hd), jnp.float32),
            pltpu.VMEM((n, rows, width), jnp.bfloat16),
            pltpu.VMEM((n, rows, width), jnp.bfloat16),
            pltpu.VMEM((1, LANES), jnp.float32),
            pltpu.VMEM((n, 1, LANES), jnp.float32),
            pltpu.SemaphoreType.DMA((6,)),
            pltpu.SemaphoreType.DMA((n,)),
            pltpu.SemaphoreType.DMA((n_seq,)),
            pltpu.SemaphoreType.DMA((n_seq,)),
            pltpu.SemaphoreType.DMA((n,)),
            pltpu.SemaphoreType.DMA((n,)),
            pltpu.SemaphoreType.DMA((n,)),
            pltpu.SemaphoreType.DMA((n,)),
        ],
        compiler_params=pltpu.CompilerParams(
            collective_id=0, has_side_effects=True, vmem_limit_bytes=67043328),
    )(queries, keys, values, lengths.T, hidden_in, out_weight, norm_gain)
    return both[0], both[1]


def fits(queries, keys, hidden_in, out_weight):
    rows, heads, hd = queries.shape
    groups, width = keys.shape[1], hidden_in.shape[1]
    n_kvh, n_seq = lax.axis_size("kvh"), lax.axis_size("seq")
    return (hd == LANES and n_kvh & (n_kvh - 1) == 0 and n_seq & (n_seq - 1) == 0 and n_kvh * n_seq % CHUNK == 0 and width % hd == 0 and (heads // groups) % max(width // hd, 1) == 0
            and rows % 2 == 0 and (rows * (width // hd)) % 16 == 0 and LANES % rows == 0
            and out_weight.shape[0] == width and out_weight.size * 2 <= 32 * 1024 * 1024)


def merged(shard, axis, combine):
    everything = jax.tree.map(lambda part: lax.all_gather(part, axis), shard)
    leading = jax.tree.map(lambda part: part[0], everything)

    def lap(k, so_far):
        return combine(so_far, jax.tree.map(lambda part: part[k], everything))

    return lax.fori_loop(1, lax.axis_size(axis), lap, leading)


def softmax_pair(first, second):
    highest = jnp.maximum(first[0], second[0])
    first_scale = jnp.exp(first[0] - highest)
    second_scale = jnp.exp(second[0] - highest)
    weight_total = first[1] * first_scale + second[1] * second_scale
    output_total = first[2] * first_scale[..., None] + second[2] * second_scale[..., None]
    return (highest, weight_total, output_total)


def body(queries, keys, values, lengths, hidden_in, out_weight, norm_gain):
    rows, heads_here, head_dim = queries.shape
    groups = keys.shape[1]
    positions = keys.shape[2]
    per_group = heads_here // groups
    query_grid = queries.reshape(rows, groups, per_group, head_dim)
    scores = jnp.einsum(
        "rkgd,rktd->rkgt", query_grid, keys, preferred_element_type=jnp.float32
    ) * head_dim ** (-0.5)
    valid = (jnp.arange(positions, dtype=jnp.int32)[None, :] < lengths)[:, None, None, :]
    peak_here = jnp.max(jnp.where(valid, scores, -jnp.inf), axis=-1)
    probs = jnp.exp(jnp.where(valid, scores - peak_here[..., None], -jnp.inf)).astype(jnp.bfloat16)
    weight_here = jnp.sum(probs, axis=-1, dtype=jnp.float32)
    partial_value = jnp.einsum("rkgt,rktd->rkgd", probs, values, preferred_element_type=jnp.float32)
    feature_width = heads_here * head_dim // lax.axis_size("seq")
    feature_start = lax.axis_index("seq") * feature_width
    highest, weight_total, output_total = merged(
        (peak_here, weight_here, partial_value), "seq", softmax_pair
    )
    whole_out = (output_total / weight_total[..., None]).reshape(rows, heads_here * head_dim)
    attention = lax.dynamic_slice_in_dim(whole_out, feature_start, feature_width, 1)
    attention = attention.astype(jnp.bfloat16)
    projected = jnp.dot(attention, out_weight, preferred_element_type=jnp.float32)
    slice_width = hidden_in.shape[1]
    slice_start = lax.axis_index(("kvh", "seq")) * slice_width
    gain_wide = norm_gain.astype(jnp.float32)
    projected_all = lax.psum(projected, ("kvh", "seq"))
    residual = lax.all_gather(hidden_in, ("kvh", "seq"), axis=1, tiled=True)
    stream_all = (residual.astype(jnp.float32) + projected_all).astype(jnp.bfloat16)
    stream_wide = stream_all.astype(jnp.float32)
    mean_square = jnp.mean(stream_wide * stream_wide, axis=1, keepdims=True)
    normed_all = (stream_wide * lax.rsqrt(mean_square + 1e-05) * gain_wide[None, :]).astype(
        jnp.bfloat16
    )
    attended = lax.dynamic_slice_in_dim(stream_all, slice_start, slice_width, 1)
    normed = lax.dynamic_slice_in_dim(normed_all, slice_start, slice_width, 1)
    return (attended, normed)


def either_body(queries, keys, values, lengths, hidden_in, out_weight, norm_gain):
    chosen = fused_body if fits(queries, keys, hidden_in, out_weight) else body
    return chosen(queries, keys, values, lengths, hidden_in, out_weight, norm_gain)


def solution(mesh):
    placed = (
        P(None, "kvh", None),
        P(None, "kvh", "seq", None),
        P(None, "kvh", "seq", None),
        P(None, "seq"),
        P(None, ("kvh", "seq")),
        P(("kvh", "seq"), None),
        P(),
    )
    return jax.shard_map(
        either_body,
        mesh=mesh,
        in_specs=placed,
        out_specs=(P(None, ("kvh", "seq")), P(None, ("kvh", "seq"))),
        check_vma=False,
    )
```

```python
import functools

import jax
import jax.numpy as jnp
from jax import lax
from jax.experimental import pallas as pl
from jax.experimental.pallas import tpu as pltpu
from jax.sharding import PartitionSpec as P

MESH = pl.DeviceIdType.MESH
LANES = 128
CHUNK = 4


def fused_kernel(dims, q_hbm, k_hbm, v_hbm, len_hbm, hid_hbm, w_hbm, gain_hbm, out_ref,
                 qv, kv, vv, lv, hv, gv, wv, send_a, recv_a, out_a, send_b, recv_b, send_c, recv_c,
                 in_sem, w_sem, sa_sem, ra_sem, sb_sem, rb_sem, sc_sem, rc_sem):
    n_kvh, n_seq, rows, heads, hd, groups, positions, width = dims
    n = n_kvh * n_seq
    per_group = heads // groups
    own_heads = width // hd
    dests = per_group // own_heads
    m = rows * own_heads
    half = m // 2
    quarter = LANES // 4
    kvh, seq = lax.axis_index("kvh"), lax.axis_index("seq")

    def flip(index, mask):
        bits = mask.bit_length()
        low = sum(lax.rem(index // (1 << i) + (mask >> i & 1), 2) * (1 << i) for i in range(bits))
        return (index // (1 << bits)) * (1 << bits) + low

    def peer(a, b):
        return flip(kvh, a), flip(seq, b)

    def hops(pair):
        return (pair[0].bit_count() + (pair[1] >> 1)), pair[0], pair[1]

    order = sorted(((a, b) for a in range(n_kvh) for b in range(n_seq)), key=hops, reverse=True)
    seq_order = sorted(range(n_seq), reverse=True)

    loads = [pltpu.make_async_copy(s, d, in_sem.at[i]) for i, (s, d) in enumerate(
        [(q_hbm, qv), (k_hbm, kv), (v_hbm, vv), (len_hbm, lv), (hid_hbm, hv),
         (gain_hbm.at[pl.ds(pl.multiple_of((kvh * n_seq + seq) * width, width), width)], gv)])]
    for load in loads[:4]:
        load.start()
    barrier = pltpu.get_barrier_semaphore()
    for a, b in order:
        if a or b:
            pl.semaphore_signal(barrier, inc=1, device_id=peer(a, b), device_id_type=MESH)

    for load in loads[4:]:
        load.start()
    w_loads = []
    for slot, (a, b) in enumerate(order):
        pa, pb = peer(a, b)
        col = pl.multiple_of((pa * n_seq + pb) * width, width)
        load = pltpu.make_async_copy(w_hbm.at[:, pl.ds(col, width)], wv.at[slot], w_sem.at[slot])
        load.start()
        w_loads.append(load)

    for load in loads[:4]:
        load.wait()
    lane = lax.broadcasted_iota(jnp.int32, (per_group, LANES), 1)
    position = lax.broadcasted_iota(jnp.int32, (per_group, positions), 1)
    for g in range(groups):
        stats = []
        for r in range(rows):
            scores = lax.dot_general(qv[r, g * per_group:(g + 1) * per_group, :], kv[r, g],
                                     (((1,), (1,)), ((), ())),
                                     preferred_element_type=jnp.float32) * hd ** (-0.5)
            valid = position < lv[0:1, r:r + 1]
            peak = jnp.max(jnp.where(valid, scores, -jnp.inf), axis=1, keepdims=True)
            probs = jnp.exp(jnp.where(valid, scores - peak, -jnp.inf)).astype(jnp.bfloat16)
            weight = jnp.sum(probs.astype(jnp.float32), axis=1, keepdims=True)
            part = jnp.dot(probs, vv[r, g], preferred_element_type=jnp.float32)
            stats.append((peak, weight))
            for j in range(dests):
                send_a[g * dests + j, r * own_heads:(r + 1) * own_heads, :] = (
                    part[j * own_heads:(j + 1) * own_heads, :])
        for rr in range(rows // 2):
            low, high = stats[rr], stats[rr + rows // 2]
            tile = jnp.where(lane < 2 * quarter,
                             jnp.where(lane < quarter, low[0], low[1]),
                             jnp.where(lane < 3 * quarter, high[0], high[1]))
            for j in range(dests):
                send_a[g * dests + j, m + rr * own_heads:m + (rr + 1) * own_heads, :] = (
                    tile[j * own_heads:(j + 1) * own_heads, :])

    pl.semaphore_wait(barrier, n - 1)
    copies = []
    for b in seq_order:
        if b:
            pa, pb = peer(0, b)
            copy = pltpu.make_async_remote_copy(
                src_ref=send_a.at[pb], dst_ref=recv_a.at[b], send_sem=sa_sem.at[b],
                recv_sem=ra_sem.at[b], device_id=(pa, pb), device_id_type=MESH)
            copy.start()
            copies.append(copy)
    recv_a[0] = send_a[seq]
    for copy in copies:
        copy.wait_recv()

    tiles = [recv_a[b, m:m + half, :] for b in range(n_seq)]
    top = functools.reduce(jnp.maximum, tiles)
    scales = [jnp.exp(tile - top) for tile in tiles]
    denom = functools.reduce(jnp.add, [
        scale * pltpu.roll(tile, LANES - quarter, 1) for scale, tile in zip(scales, tiles)])
    for h in range(2):
        at = h * 2 * quarter
        numer = functools.reduce(jnp.add, [
            scales[b][:, at:at + 1] * recv_a[b, h * half:(h + 1) * half, :] for b in range(n_seq)])
        out_a[h * half:(h + 1) * half, :] = numer / denom[:, at:at + 1]
    attention = jnp.concatenate(
        [out_a[pl.ds(i, rows, stride=own_heads), :] for i in range(own_heads)], axis=1
    ).astype(jnp.bfloat16)

    for first in range(0, n, CHUNK):
        slots = range(first, first + CHUNK)
        for slot in slots:
            w_loads[slot].wait()
        products = [jnp.dot(attention, wv[slot], preferred_element_type=jnp.float32)
                    for slot in slots]
        for slot, product in zip(slots, products):
            if slot < n - 1:
                send_b[slot] = product.astype(send_b.dtype)
        for slot in slots:
            if slot < n - 1:
                copy = pltpu.make_async_remote_copy(
                    src_ref=send_b.at[slot], dst_ref=recv_b.at[slot], send_sem=sb_sem.at[slot],
                    recv_sem=rb_sem.at[slot], device_id=peer(*order[slot]), device_id_type=MESH)
                copy.start()
                copies.append(copy)
    own = products[-1]
    loads[4].wait()
    total = own + hv[...].astype(jnp.float32)
    for first in range(0, n - 1, 8):
        group = range(first, min(first + 8, n - 1))
        for slot in group:
            copies[n_seq - 1 + slot].wait_recv()
        for slot in group:
            total = total + recv_b[slot].astype(jnp.float32)
    attended = total.astype(jnp.bfloat16)
    out_ref[0] = attended
    stream = attended.astype(jnp.float32)
    squares = jnp.sum(stream * stream, axis=1, keepdims=True)
    lane_one = lax.broadcasted_iota(jnp.int32, (1, LANES), 1)
    packed = jnp.zeros((1, LANES), jnp.float32)
    share = LANES // rows
    for r in range(rows):
        packed = jnp.where(lane_one // share == r, squares[r:r + 1, :], packed)
    send_c[...] = packed
    last = []
    for slot, (a, b) in enumerate(order):
        if a or b:
            copy = pltpu.make_async_remote_copy(
                src_ref=send_c, dst_ref=recv_c.at[slot], send_sem=sc_sem.at[slot],
                recv_sem=rc_sem.at[slot], device_id=peer(a, b), device_id_type=MESH)
            copy.start()
            last.append(copy)
    loads[5].wait()
    gain_wide = gv[...].astype(jnp.float32).reshape(1, width)
    for copy in last:
        copy.wait_recv()
    for slot in range(n - 1):
        packed = packed + recv_c[slot]
    scale = lax.rsqrt(packed / (n * width) + 1e-05)
    for r in range(rows):
        out_ref[1, r:r + 1, :] = (
            stream[r:r + 1, :] * scale[:, r * share:r * share + 1] * gain_wide
        ).astype(jnp.bfloat16)
    for copy in copies + last:
        copy.wait_send()


def fused_body(queries, keys, values, lengths, hidden_in, out_weight, norm_gain):
    rows, heads, hd = queries.shape
    groups, positions = keys.shape[1], keys.shape[2]
    n_kvh, n_seq = lax.axis_size("kvh"), lax.axis_size("seq")
    n = n_kvh * n_seq
    width = hidden_in.shape[1]
    own_heads = width // hd
    m = rows * own_heads
    message = m + m // 2
    dims = (n_kvh, n_seq, rows, heads, hd, groups, positions, width)
    hbm = pl.BlockSpec(memory_space=pltpu.HBM)
    vmem = pl.BlockSpec(memory_space=pltpu.VMEM)
    both = pl.pallas_call(
        functools.partial(fused_kernel, dims),
        out_shape=jax.ShapeDtypeStruct((2, rows, width), jnp.bfloat16),
        in_specs=[hbm] * 7,
        out_specs=vmem,
        scratch_shapes=[
            pltpu.VMEM(queries.shape, queries.dtype),
            pltpu.VMEM(keys.shape, keys.dtype),
            pltpu.VMEM(values.shape, values.dtype),
            pltpu.VMEM(lengths.T.shape, lengths.dtype),
            pltpu.VMEM(hidden_in.shape, hidden_in.dtype),
            pltpu.VMEM((width,), norm_gain.dtype),
            pltpu.VMEM((n, out_weight.shape[0], width), out_weight.dtype),
            pltpu.VMEM((n_seq, message, hd), jnp.float32),
            pltpu.VMEM((n_seq, message, hd), jnp.float32),
            pltpu.VMEM((m, hd), jnp.float32),
            pltpu.VMEM((n, rows, width), jnp.bfloat16),
            pltpu.VMEM((n, rows, width), jnp.bfloat16),
            pltpu.VMEM((1, LANES), jnp.float32),
            pltpu.VMEM((n, 1, LANES), jnp.float32),
            pltpu.SemaphoreType.DMA((6,)),
            pltpu.SemaphoreType.DMA((n,)),
            pltpu.SemaphoreType.DMA((n_seq,)),
            pltpu.SemaphoreType.DMA((n_seq,)),
            pltpu.SemaphoreType.DMA((n,)),
            pltpu.SemaphoreType.DMA((n,)),
            pltpu.SemaphoreType.DMA((n,)),
            pltpu.SemaphoreType.DMA((n,)),
        ],
        compiler_params=pltpu.CompilerParams(
            collective_id=0, has_side_effects=True, vmem_limit_bytes=40 * 1024 * 1024),
    )(*(pltpu.with_memory_space_constraint(operand, pltpu.HBM) for operand in (
        queries, keys, values, lengths.T, hidden_in, out_weight, norm_gain)))
    return both[0], both[1]


def fits(queries, keys, hidden_in, out_weight):
    rows, heads, hd = queries.shape
    groups, width = keys.shape[1], hidden_in.shape[1]
    n_kvh, n_seq = lax.axis_size("kvh"), lax.axis_size("seq")
    return (hd == LANES and n_kvh & (n_kvh - 1) == 0 and n_seq & (n_seq - 1) == 0 and n_kvh * n_seq % CHUNK == 0 and width % hd == 0 and (heads // groups) % max(width // hd, 1) == 0
            and rows % 2 == 0 and (rows * (width // hd)) % 16 == 0 and LANES % rows == 0
            and out_weight.shape[0] == width and out_weight.size * 2 <= 32 * 1024 * 1024)


def merged(shard, axis, combine):
    everything = jax.tree.map(lambda part: lax.all_gather(part, axis), shard)
    leading = jax.tree.map(lambda part: part[0], everything)

    def lap(k, so_far):
        return combine(so_far, jax.tree.map(lambda part: part[k], everything))

    return lax.fori_loop(1, lax.axis_size(axis), lap, leading)


def softmax_pair(first, second):
    highest = jnp.maximum(first[0], second[0])
    first_scale = jnp.exp(first[0] - highest)
    second_scale = jnp.exp(second[0] - highest)
    weight_total = first[1] * first_scale + second[1] * second_scale
    output_total = first[2] * first_scale[..., None] + second[2] * second_scale[..., None]
    return (highest, weight_total, output_total)


def body(queries, keys, values, lengths, hidden_in, out_weight, norm_gain):
    rows, heads_here, head_dim = queries.shape
    groups = keys.shape[1]
    positions = keys.shape[2]
    per_group = heads_here // groups
    query_grid = queries.reshape(rows, groups, per_group, head_dim)
    scores = jnp.einsum(
        "rkgd,rktd->rkgt", query_grid, keys, preferred_element_type=jnp.float32
    ) * head_dim ** (-0.5)
    valid = (jnp.arange(positions, dtype=jnp.int32)[None, :] < lengths)[:, None, None, :]
    peak_here = jnp.max(jnp.where(valid, scores, -jnp.inf), axis=-1)
    probs = jnp.exp(jnp.where(valid, scores - peak_here[..., None], -jnp.inf)).astype(jnp.bfloat16)
    weight_here = jnp.sum(probs, axis=-1, dtype=jnp.float32)
    partial_value = jnp.einsum("rkgt,rktd->rkgd", probs, values, preferred_element_type=jnp.float32)
    feature_width = heads_here * head_dim // lax.axis_size("seq")
    feature_start = lax.axis_index("seq") * feature_width
    highest, weight_total, output_total = merged(
        (peak_here, weight_here, partial_value), "seq", softmax_pair
    )
    whole_out = (output_total / weight_total[..., None]).reshape(rows, heads_here * head_dim)
    attention = lax.dynamic_slice_in_dim(whole_out, feature_start, feature_width, 1)
    attention = attention.astype(jnp.bfloat16)
    projected = jnp.dot(attention, out_weight, preferred_element_type=jnp.float32)
    slice_width = hidden_in.shape[1]
    slice_start = lax.axis_index(("kvh", "seq")) * slice_width
    gain_wide = norm_gain.astype(jnp.float32)
    projected_all = lax.psum(projected, ("kvh", "seq"))
    residual = lax.all_gather(hidden_in, ("kvh", "seq"), axis=1, tiled=True)
    stream_all = (residual.astype(jnp.float32) + projected_all).astype(jnp.bfloat16)
    stream_wide = stream_all.astype(jnp.float32)
    mean_square = jnp.mean(stream_wide * stream_wide, axis=1, keepdims=True)
    normed_all = (stream_wide * lax.rsqrt(mean_square + 1e-05) * gain_wide[None, :]).astype(
        jnp.bfloat16
    )
    attended = lax.dynamic_slice_in_dim(stream_all, slice_start, slice_width, 1)
    normed = lax.dynamic_slice_in_dim(normed_all, slice_start, slice_width, 1)
    return (attended, normed)


def either_body(queries, keys, values, lengths, hidden_in, out_weight, norm_gain):
    chosen = fused_body if fits(queries, keys, hidden_in, out_weight) else body
    return chosen(queries, keys, values, lengths, hidden_in, out_weight, norm_gain)


def solution(mesh):
    placed = (
        P(None, "kvh", None),
        P(None, "kvh", "seq", None),
        P(None, "kvh", "seq", None),
        P(None, "seq"),
        P(None, ("kvh", "seq")),
        P(("kvh", "seq"), None),
        P(),
    )
    return jax.shard_map(
        either_body,
        mesh=mesh,
        in_specs=placed,
        out_specs=(P(None, ("kvh", "seq")), P(None, ("kvh", "seq"))),
        check_vma=False,
    )
```
